32 devices in a mesh: layer: 2 (over y), feat: 4 (over x, core), width: 4 (over z).
Axes of the slice: x: 2, y: 2, z: 4, core: 2. Of those that a mesh axis runs over, the one named last changes fastest.
Arguments:
- resid: bfloat16 [2, 128, 2048], P(None, 'layer', 'width'), may hold values from -6 to 6
- enc_w: bfloat16 [2, 2048, 65536], P(None, 'width', ('layer', 'feat')), may hold values from -0.125 to 0.125
- enc_b: float32 [2, 65536], P(None, ('layer', 'feat')), may hold values from -3 to 3
- dec_w: float32 [3, 65536, 2048], P(None, ('layer', 'feat'), 'width'), may hold values from -0.03125 to 0.03125
- dec_b: float32 [2, 2048], P(None, 'width'), may hold values from -2 to 2
- target: float32 [2, 128, 2048], P(None, ('layer', 'feat'), 'width'), may hold values from -6 to 6
Outputs:
- recon: float32 [2, 128, 2048], P(None, ('layer', 'feat'), 'width')
- err: float32 [2, 128], P(None, ('layer', 'feat'))
The draws below stay inside these ranges and needn't reach their ends.
All inputs are finite; a program needn't handle non-finite values.
Results may differ from the reference program's by a relative error of at most 0.00035.
Values may be sent and summed in bfloat16 or wider, within the bound.
No kernel may reach another device: no remote copies, remote signals or barrier semaphores. Data moves between devices by JAX's collectives and lax.ppermute only.
A program may use at most 128 MiB of HBM per device.

```python
import jax
import jax.numpy as jnp
from jax import lax

D = 2048
FEATURES = 65536
LAYERS = 2
TOKENS = 128
BLOCKS = 3


def raised(array, own_key, source, target, shards_of, factor):
    owner, partner = [(jnp.arange(array.shape[position]) // (array.shape[position] // shards_of)).reshape([-1 if axis == position else 1 for axis in range(array.ndim)]) for position in (source, target)]
    chosen = jax.random.permutation(own_key, shards_of)[partner]
    strong = (owner == chosen) | (owner == (partner + shards_of // 2) % shards_of)
    return jnp.where(strong, factor * array, array)


def block_scale(rng, shape, split, low, top_value):
    level = 1.0
    for position, shards_of in split:
        heights = jax.random.uniform(jax.random.fold_in(jax.random.fold_in(rng, 6), position), (shards_of,), jnp.float32, low / len(split), top_value / len(split))
        level = level * jnp.repeat(jnp.exp(heights), shape[position] // shards_of).reshape((-1,) + (1,) * (len(shape) - 1 - position))
    return level


def scatter_about(stream_key, dims, width, bound, split=(), kind=jnp.bfloat16):
    level = block_scale(stream_key, dims, split, -0.22, 0.18) if split else 1.0
    result = jax.random.normal(stream_key, dims, jnp.float32) * width * level
    return jnp.minimum(jnp.maximum(result, -bound), bound).astype(kind)


def heavy_noise(key, extent, spread, reach, cuts, heavy, dtype=jnp.bfloat16):
    result = spread * jax.random.normal(key, extent, jnp.float32)
    if cuts:
        result = result * block_scale(key, extent, cuts, -0.22, 0.18)
    return jnp.clip(raised(result, jax.random.fold_in(key, 3), *heavy), -reach, reach).astype(dtype)


def setup_inputs(seed: int = 0) -> dict:
    arg_keys = jax.random.split(jax.random.key(seed), 7)
    return {
        "resid": scatter_about(arg_keys[0], (LAYERS, TOKENS, D), 1.0, 6.0, ((1, 2), (2, 4))),
        "enc_w": scatter_about(arg_keys[1], (LAYERS, D, FEATURES), D ** -0.5, 0.125, ((1, 4), (2, 8))),
        "enc_b": scatter_about(arg_keys[2], (LAYERS, FEATURES), 0.5, 3.0, ((1, 8),), jnp.float32),
        "dec_w": heavy_noise(arg_keys[3], (BLOCKS, FEATURES, D), FEATURES ** -0.5, 0.03125, ((1, 8), (2, 4)), (1, 2, 8, 2.0), jnp.float32),
        "dec_b": scatter_about(arg_keys[4], (LAYERS, D), 0.3, 2.0, ((1, 4),), jnp.float32),
        "target": scatter_about(arg_keys[5], (LAYERS, TOKENS, D), 1.0, 6.0, ((1, 8), (2, 4)), jnp.float32),
    }


def reference(resid, enc_w, enc_b, dec_w, dec_b, target):
    acts = []
    for layer_idx in range(LAYERS):
        pre = jnp.dot(resid[layer_idx], enc_w[layer_idx], preferred_element_type=jnp.float32) + enc_b[layer_idx][None, :]
        acts.append(jnp.maximum(pre, 0.0))
    outs = []
    for target_idx in range(LAYERS):
        total = jnp.zeros((TOKENS, D), jnp.float32) + dec_b[target_idx][None, :]
        for layer_idx in range(target_idx + 1):
            block = target_idx * (target_idx + 1) // 2 + layer_idx
            total = total + jnp.dot(acts[layer_idx], dec_w[block], precision=lax.Precision.HIGHEST, preferred_element_type=jnp.float32)
        outs.append(total)
    recon = jnp.stack(outs, 0)
    diff = recon - target
    err = jnp.sum(diff * diff, axis=2) / (jnp.sum(target * target, axis=2) + 1e-6)
    return recon, err
```

```python
import math

import jax
import jax.numpy as jnp
from jax import lax
from jax.sharding import PartitionSpec as P

RESID_MAX = 6.0
ENC_MAX = 0.125
F16_MAX = 65504.0


def chunk_bounds(features, parts):
    unit = features // sum(parts)
    bounds, start = [], 0
    for part in parts:
        bounds.append((start, start + part * unit))
        start += part * unit
    return bounds


def halving(rows, axis):
    size = lax.axis_size(axis)
    me = lax.axis_index(axis)
    bit = 1
    blocks = rows.reshape((size, rows.shape[0] // size) + rows.shape[1:])
    count = size
    while count > 1:
        pairs = blocks.reshape((count // 2, 2) + blocks.shape[1:])
        mine = (me // bit) % 2
        keep = lax.dynamic_index_in_dim(pairs, mine, 1, keepdims=False)
        give = lax.dynamic_index_in_dim(pairs, 1 - mine, 1, keepdims=False)
        got = lax.ppermute(give, axis, [(i, i ^ bit) for i in range(size)])
        blocks = keep + got
        bit *= 2
        count //= 2
    return blocks[0]


def butterfly(value, axis):
    size = lax.axis_size(axis)
    bit = 1
    while bit < size:
        value = value + lax.ppermute(value, axis, [(i, i ^ bit) for i in range(size)])
        bit *= 2
    return value


def gather_tokens(resid, axis):
    size = lax.axis_size(axis)
    if size != 2:
        return lax.all_gather(resid, axis, axis=1, tiled=True)
    other = lax.ppermute(resid, axis, [(0, 1), (1, 0)])
    first = lax.axis_index(axis) == 0
    return jnp.concatenate(
        [jnp.where(first, resid, other), jnp.where(first, other, resid)], axis=1
    )


def per_device(resid, enc_w, enc_b, dec_w, dec_b, target):
    layers, _, width = resid.shape
    features = enc_w.shape[2]
    size = lax.axis_size("width")
    scale = 2.0 ** math.floor(math.log2(F16_MAX / (width * size * RESID_MAX * ENC_MAX)))
    gathered = gather_tokens(resid, "layer") * jnp.asarray(scale, resid.dtype)
    tokens = gathered.shape[1]

    work = []
    for layer in range(layers):
        parts = (1, 1, 2, 2, 2) if layer == 0 else (2, 2, 2, 1, 1)
        work += [(layer, lo, hi) for lo, hi in chunk_bounds(features, parts)]

    partial, received = [], []
    for layer, lo, hi in work:
        partial.append(
            jnp.dot(gathered[layer], enc_w[layer, :, lo:hi], preferred_element_type=jnp.float32)
        )
        received.append({})

    def exchange(k, j):
        value = partial[k]
        if j > 1:
            value = value + received[k][j - 1].astype(jnp.float32)
        received[k][j] = lax.ppermute(
            value.astype(jnp.float16), "width", [(j - 1, j), (size - j, size - j - 1)]
        )

    count = len(work)
    for stage in range(count + size - 2):
        for j in range(1, size):
            if 0 <= stage - j + 1 < count:
                exchange(stage - j + 1, j)

    recon = [None] * layers
    for k, (layer, lo, hi) in enumerate(work):
        total = partial[k]
        for j in range(1, size):
            total = total + received[k][j].astype(jnp.float32)
        act = jnp.maximum(total + scale * enc_b[layer, lo:hi], 0.0)
        for m in range(layer, layers):
            block = m * (m + 1) // 2 + layer
            term = jnp.dot(
                act, dec_w[block, lo:hi], precision=lax.Precision.HIGH,
                preferred_element_type=jnp.float32,
            )
            recon[m] = term if recon[m] is None else recon[m] + term

    outs, errs = [], []
    for m in range(layers):
        rows = recon[m].reshape(lax.axis_size("layer"), -1, recon[m].shape[1])
        rows = rows.transpose(1, 0, 2)
        rows = halving(rows, "feat").transpose(1, 0, 2)
        rows = halving(rows.reshape((-1,) + rows.shape[2:]), "layer")
        out = rows * (1.0 / scale) + dec_b[m]
        diff = out - target[m]
        sums = jnp.stack([jnp.sum(diff * diff, axis=1), jnp.sum(target[m] * target[m], axis=1)])
        sums = butterfly(sums, "width")
        outs.append(out)
        errs.append(sums[0] / (sums[1] + 1e-06))
    return jnp.stack(outs), jnp.stack(errs)


def solution(mesh):
    in_specs = (
        P(None, "layer", "width"),
        P(None, "width", ("layer", "feat")),
        P(None, ("layer", "feat")),
        P(None, ("layer", "feat"), "width"),
        P(None, "width"),
        P(None, ("layer", "feat"), "width"),
    )
    out_specs = (P(None, ("layer", "feat"), "width"), P(None, ("layer", "feat")))
    return jax.shard_map(
        per_device, mesh=mesh, in_specs=in_specs, out_specs=out_specs, check_vma=False
    )
```

```python
import functools
import math

import jax
import jax.numpy as jnp
from jax import lax
from jax.experimental import pallas as pl
from jax.experimental.pallas import tpu as pltpu
from jax.sharding import PartitionSpec as P


RESID_MAX = 6.0
ENC_MAX = 0.125
F16_MAX = 65504.0
LAG = 3
VMEM_LIMIT = 20 << 20
WIDTHS = ((14, 12, 12, 14, 12), (12, 14, 12, 12, 14))


def chunk_list(layers, features):
    units = features // 64
    widths = WIDTHS if features % (64 * 128) == 0 and layers == 2 else ((16,) * 4,) * layers
    work = []
    for layer in range(layers):
        start = 0
        for width in widths[layer]:
            work.append((layer, start * units, (start + width) * units))
            start += width
    return work


def schedule(count):
    ops = [("work", 0)]
    for stage in range(count + LAG + 1):
        if stage < count + LAG:
            ops.append(("outer", stage))
        if 0 <= stage - 1 < count:
            ops.append(("inner", stage - 1))
        if stage + 1 < count or 0 <= stage - 1 - LAG < count:
            ops.append(("work", stage + 1))
    return ops


def work_kernel(enc_at, dec_at, pieces, scale, *refs):
    refs = list(refs)
    if enc_at is not None:
        rows_ref, enc_ref = refs[:2]
        del refs[:2]
    if dec_at is not None:
        base_ref, last_ref, bias_ref, dec_ref, sum_ref = refs[:5]
        del refs[:5]
    if enc_at is not None:
        pre_ref = refs.pop(0)
    if dec_at is not None:
        out_ref = refs.pop(0)
    if enc_at is not None:
        enc_buf, enc_sem = refs[:2]
        del refs[:2]
        layer, start, stop = enc_at
        enc_copy = pltpu.make_async_copy(
            enc_ref.at[layer, :, pl.ds(start, stop - start)], enc_buf, enc_sem
        )
        enc_copy.start()
    if dec_at is not None:
        act_ref, dec_buf, dec_sem = refs
        layer, start, stop = dec_at
        targets, tokens, _ = out_ref.shape
        depth = (stop - start) // pieces
        copies = []
        for m in range(targets):
            target = m + layer
            for piece in range(pieces):
                copy = pltpu.make_async_copy(
                    dec_ref.at[
                        target * (target + 1) // 2 + layer, pl.ds(start + piece * depth, depth)
                    ],
                    dec_buf.at[m * pieces + piece],
                    dec_sem.at[m * pieces + piece],
                )
                copy.start()
                copies.append(copy)
    if enc_at is not None:
        enc_copy.wait()
        pre_ref[...] = jnp.dot(rows_ref[0], enc_buf[...], preferred_element_type=jnp.float32)
    if dec_at is not None:
        bias = bias_ref[layer : layer + 1, start:stop] * scale
        act = jnp.maximum(base_ref[...] + last_ref[...] + bias, 0.0)
        high = act.astype(jnp.bfloat16)
        act_ref[:tokens] = high
        act_ref[tokens:] = (act - high.astype(jnp.float32)).astype(jnp.bfloat16)
        for m in range(targets):
            total = sum_ref[m]
            for piece in range(pieces):
                copies[m * pieces + piece].wait()
                weights = dec_buf[m * pieces + piece]
                high = weights.astype(jnp.bfloat16)
                low = (weights - high.astype(jnp.float32)).astype(jnp.bfloat16)
                part = act_ref[:, piece * depth : (piece + 1) * depth]
                both = jnp.dot(part, high, preferred_element_type=jnp.float32)
                rest = jnp.dot(part[:tokens], low, preferred_element_type=jnp.float32)
                total = total + (both[:tokens] + both[tokens:] + rest)
            out_ref[m] = total


def work_call(rows, enc_w, pre, bias, dec_w, sums, enc_at, dec_at, scale):
    operands, in_specs, out_specs, out_shape, scratch = [], [], [], [], []
    flops = moved = pieces = 0
    if enc_at is not None:
        layer, start, stop = enc_at
        _, tokens, width = rows.shape
        operands += [rows, pltpu.with_memory_space_constraint(enc_w, pltpu.HBM)]
        in_specs += [
            pl.BlockSpec((1, tokens, width), lambda i: (layer, 0, 0)),
            pl.BlockSpec(memory_space=pltpu.HBM),
        ]
        out_specs.append(pl.BlockSpec((tokens, stop - start), lambda i: (0, 0)))
        out_shape.append(jax.ShapeDtypeStruct((tokens, stop - start), jnp.float32))
        scratch += [
            pltpu.VMEM((width, stop - start), enc_w.dtype), pltpu.SemaphoreType.DMA,
        ]
        flops += 2 * tokens * width * (stop - start)
        moved += 2 * width * (stop - start)
    if dec_at is not None:
        _, low, high = dec_at
        targets, tokens, width = sums.shape
        pieces = 2 if (high - low) % 256 == 0 else 1
        operands += [*pre, bias, pltpu.with_memory_space_constraint(dec_w, pltpu.HBM), sums]
        in_specs += [
            pl.BlockSpec(pre[0].shape, lambda i: (0, 0)),
            pl.BlockSpec(pre[1].shape, lambda i: (0, 0)),
            pl.BlockSpec(bias.shape, lambda i: (0, 0)),
            pl.BlockSpec(memory_space=pltpu.HBM),
            pl.BlockSpec(sums.shape, lambda i: (0, 0, 0)),
        ]
        out_specs.append(pl.BlockSpec(sums.shape, lambda i: (0, 0, 0)))
        out_shape.append(jax.ShapeDtypeStruct(sums.shape, jnp.float32))
        scratch += [
            pltpu.VMEM((2 * tokens, high - low), jnp.bfloat16),
            pltpu.VMEM((targets * pieces, (high - low) // pieces, width), dec_w.dtype),
            pltpu.SemaphoreType.DMA((targets * pieces,)),
        ]
        flops += 6 * tokens * width * (high - low) * targets
        moved += 4 * width * (high - low) * targets
    outs = pl.pallas_call(
        functools.partial(work_kernel, enc_at, dec_at, pieces, scale),
        grid=(1,),
        in_specs=in_specs,
        out_specs=out_specs,
        out_shape=out_shape,
        scratch_shapes=scratch,
        compiler_params=pltpu.CompilerParams(vmem_limit_bytes=VMEM_LIMIT),
        cost_estimate=pl.CostEstimate(flops=flops, bytes_accessed=moved, transcendentals=0),
    )(*operands)
    return (outs[0] if enc_at is not None else None, outs[-1] if dec_at is not None else None)


def halving(rows, axis):
    size = lax.axis_size(axis)
    me = lax.axis_index(axis)
    bit = 1
    blocks = rows.reshape((size, rows.shape[0] // size) + rows.shape[1:])
    count = size
    while count > 1:
        pairs = blocks.reshape((count // 2, 2) + blocks.shape[1:])
        mine = (me // bit) % 2
        keep = lax.dynamic_index_in_dim(pairs, mine, 1, keepdims=False)
        give = lax.dynamic_index_in_dim(pairs, 1 - mine, 1, keepdims=False)
        got = lax.ppermute(give, axis, [(i, i ^ bit) for i in range(size)])
        blocks = keep + got
        bit *= 2
        count //= 2
    return blocks[0]


def butterfly(value, axis):
    size = lax.axis_size(axis)
    bit = 1
    while bit < size:
        value = value + lax.ppermute(value, axis, [(i, i ^ bit) for i in range(size)])
        bit *= 2
    return value


def gather_tokens(resid, axis):
    size = lax.axis_size(axis)
    if size != 2:
        return lax.all_gather(resid, axis, axis=1, tiled=True)
    other = lax.ppermute(resid, axis, [(0, 1), (1, 0)])
    first = lax.axis_index(axis) == 0
    return jnp.concatenate(
        [jnp.where(first, resid, other), jnp.where(first, other, resid)], axis=1
    )


def per_device(resid, enc_w, enc_b, dec_w, dec_b, target):
    layers, _, width = resid.shape
    features = enc_w.shape[2]
    size = lax.axis_size("width")
    scale = 2.0 ** math.floor(math.log2(F16_MAX / (width * size * RESID_MAX * ENC_MAX)))
    gathered = gather_tokens(resid, "layer") * jnp.asarray(scale, resid.dtype)
    tokens = gathered.shape[1]
    work = chunk_list(layers, features)
    place = lax.axis_index("width")
    outside = (place == 0) | (place == size - 1)
    partial, base, outer, inner = {}, {}, {}, {}
    sums = jnp.zeros((layers, tokens, dec_w.shape[2]), jnp.float32)
    recon = [None] * layers
    for kind, k in schedule(len(work)):
        if kind == "work":
            enc_at = work[k] if k < len(work) else None
            done = k - 2 - LAG
            dec_at = work[done] if 0 <= done < len(work) else None
            pre = None
            if dec_at is not None:
                last = jnp.where(
                    outside,
                    outer[done + LAG].astype(jnp.float32),
                    inner[done].astype(jnp.float32),
                )
                pre = (base[done], last)
            partial[k], new_sums = work_call(
                gathered, enc_w, pre, enc_b, dec_w, sums, enc_at, dec_at, scale
            )
            if dec_at is not None:
                layer, sums = dec_at[0], new_sums
                if done + 1 == len(work) or work[done + 1][0] > layer:
                    recon[layer] = sums[0]
                    sums = sums[1:]
        elif kind == "outer":
            pairs = []
            if k < len(work):
                pairs += [(0, 1), (3, 2)]
                value = partial[k]
            if k >= LAG:
                pairs += [(1, 0), (2, 3)]
                back = partial[k - LAG] + inner[k - LAG].astype(jnp.float32)
                value = jnp.where(outside, value, back) if k < len(work) else back
            outer[k] = lax.ppermute(value.astype(jnp.float16), "width", pairs)
        else:
            value = partial[k] + outer[k].astype(jnp.float32)
            base[k] = jnp.where(outside, partial[k], value)
            inner[k] = lax.ppermute(value.astype(jnp.float16), "width", [(1, 2), (2, 1)])

    outs, errs = [], []
    for m in range(layers):
        rows = recon[m].reshape(lax.axis_size("layer"), -1, recon[m].shape[1])
        rows = rows.transpose(1, 0, 2)
        rows = halving(rows, "feat").transpose(1, 0, 2)
        rows = halving(rows.reshape((-1,) + rows.shape[2:]), "layer")
        out = rows * (1.0 / scale) + dec_b[m]
        diff = out - target[m]
        sq = jnp.stack([jnp.sum(diff * diff, axis=1), jnp.sum(target[m] * target[m], axis=1)])
        sq = butterfly(sq, "width")
        outs.append(out)
        errs.append(sq[0] / (sq[1] + 1e-06))
    return jnp.stack(outs), jnp.stack(errs)


def solution(mesh):
    in_specs = (
        P(None, "layer", "width"),
        P(None, "width", ("layer", "feat")),
        P(None, ("layer", "feat")),
        P(None, ("layer", "feat"), "width"),
        P(None, "width"),
        P(None, ("layer", "feat"), "width"),
    )
    out_specs = (P(None, ("layer", "feat"), "width"), P(None, ("layer", "feat")))

    return jax.shard_map(
        per_device, mesh=mesh, in_specs=in_specs, out_specs=out_specs, check_vma=False
    )
```
